32 devices in a mesh: dp: 4 (over x, core), expert: 8 (over z, y).
Axes of the slice: x: 2, y: 2, z: 4, core: 2. Of those that a mesh axis runs over, the one named last changes fastest.
Arguments:
- x_online: bfloat16 [4096, 2048], P(('dp', 'expert')), may hold values from -6 to 6
- x_target: bfloat16 [4096, 2048], P(('dp', 'expert')), may hold values from -6 to 6
- routes: int32 [4096, 2], P(('dp', 'expert')), may hold values from 0 to 15, all different within a row; in each aligned block of 128 rows (0 to 127, 128 to 255, ...) at most 32 rows name the same one
- gate_probs: float32 [4096, 2], P(('dp', 'expert')), may hold values from 0.2 to 1
- expert_place: int32 [16], replicated, may hold values from 0 to 15, each once
- gate_online: bfloat16 [32, 2048, 256], P(('dp', 'expert')), may hold values from -0.125 to 0.125
- up_online: bfloat16 [32, 2048, 256], P(('dp', 'expert')), may hold values from -0.125 to 0.125
- down_online: bfloat16 [32, 256, 2048], P(('dp', 'expert')), may hold values from -0.25 to 0.25
- gate_target: bfloat16 [32, 2048, 256], P(('dp', 'expert')), may hold values from -0.125 to 0.125
- up_target: bfloat16 [32, 2048, 256], P(('dp', 'expert')), may hold values from -0.125 to 0.125
- down_target: bfloat16 [32, 256, 2048], P(('dp', 'expert')), may hold values from -0.25 to 0.25
Outputs:
- input_grad: bfloat16 [4096, 2048], P(('dp', 'expert'))
- grad_gate: bfloat16 [32, 2048, 256], P(('dp', 'expert'))
- grad_up: bfloat16 [32, 2048, 256], P(('dp', 'expert'))
- grad_down: bfloat16 [32, 256, 2048], P(('dp', 'expert'))
The draws below stay inside these ranges and needn't reach their ends.
Inputs may be any that keep to these rules, and one draw needn't show every extreme that they name: `routes`: each row names two different experts. Among the 128 rows of one device no expert is named more than 32 times, and in every draw some expert is named exactly 32 times by the rows of some device. `expert_place`: A permutation: each expert has a place of its own.
All inputs are finite; a program needn't handle non-finite values.
Results may differ from the reference program's by a relative error of at most 0.011.
Values may be sent and summed in bfloat16 or wider, within the bound.
A program may use at most 128 MiB of HBM per device.

```python
import math
import jax
import jax.numpy as jnp
import numpy as np
from jax import lax

D = 2048
FF = 512
TOK_DEV = 128
EXPERTS = 16
UNITS = 32
FF_HALF = 256
CAP = 32
TOKENS = 4096
N_DP = 4
N_EXPERT = 8


def levels(rng, shape, shards, least, high):
    factor_of, own = 1.0, jax.random.fold_in(rng, 6)
    for dim, shards_of in shards:
        draws = jnp.exp(jax.random.uniform(jax.random.fold_in(own, dim), (shards_of,), jnp.float32, least / len(shards), high / len(shards)))
        factor_of = factor_of * jnp.repeat(draws, shape[dim] // shards_of).reshape([-1 if axis == dim else 1 for axis in range(len(shape))])
    return factor_of


def assign_block(own_key, own, number, rows, amount, top, bound, skew):
    sequence = jax.random.permutation(own_key, amount)
    packed, usual = load_shares(amount, rows * top, bound, skew, True), load_shares(amount, rows * top, bound, skew, False)
    places = jnp.arange(amount)

    def named(sizes, turn):
        used = int((sizes > 0).sum())
        fixed = max(1, used // 4)
        passed = fixed + (places - fixed + turn * (used - fixed)) % max(1, amount - fixed)
        return jnp.zeros((amount,), jnp.int32).at[sequence[jnp.where(places < fixed, places, passed)]].set(jnp.asarray(sizes, jnp.int32))

    sizes = jnp.where(number % 4 == 0, named(packed, number // 4), named(usual, number - number // 4 - 1))
    mixed = jax.random.permutation(jax.random.fold_in(own, 3), amount)
    source_of, taker = mixed[0:amount // 2 * 2:2], mixed[1:amount // 2 * 2:2]
    slack = jnp.minimum(sizes[source_of] - 1, bound - sizes[taker]) // 2
    slack = jnp.where((source_of == sequence[0]) | (taker == sequence[0]) | (sizes[taker] == 0), 0, jnp.maximum(slack, 0))
    passed = jax.random.randint(jax.random.fold_in(own, 4), (amount // 2,), 0, 1 << 20) % (slack + 1)
    sizes = sizes.at[source_of].add(-passed).at[taker].add(passed)
    items = jnp.searchsorted(jnp.cumsum(sizes), jnp.arange(rows * top), side="right").astype(jnp.int32)
    listing = items.reshape(top, rows).T
    listing = listing[jax.random.permutation(jax.random.fold_in(own, 1), rows)]
    turn = jax.random.randint(jax.random.fold_in(own, 2), (rows, 1), 0, top)
    return jnp.take_along_axis(listing, (jnp.arange(top)[None, :] + turn) % top, axis=1)


def load_shares(count, total, limit, slope, full):
    loads = [(1 << 20) // math.isqrt(rank ** slope) + 1 for rank in range(1, count + 1)]
    largest = limit if full else min(limit, max(-(-total // count), total * loads[0] // sum(loads)))
    least = 1 if total - largest >= count - 1 else 0
    counts, surplus = [largest] + [least] * (count - 1), total - largest - least * (count - 1)
    while surplus > 0:
        candidates = [i for i in range(1, count) if counts[i] < largest] or [i for i in range(1, count) if counts[i] < limit]
        pool, budget = sum([loads[i] for i in candidates]), surplus
        for i in candidates:
            more = min(limit - counts[i], max(1, budget * loads[i] // pool), surplus)
            counts[i] = counts[i] + more
            surplus = surplus - more
    return np.array(counts)


def noise(rng, dims, spread, most, shards=(), kind=jnp.bfloat16):
    drawn = spread * jax.random.normal(rng, dims, jnp.float32)
    if shards:
        drawn = drawn * levels(rng, dims, shards, -0.22, 0.18)
    return jnp.clip(drawn, -most, most).astype(kind)


def setup_inputs(seed: int = 0) -> dict:
    splits = jax.random.split(jax.random.key(seed), 12)
    x_online = noise(splits[0], (TOKENS, D), 1.0, 6.0, ((0, 32),))
    x_target = noise(splits[1], (TOKENS, D), 1.0, 6.0, ((0, 32),))
    routes_keys = jax.random.split(jax.random.fold_in(splits[2], 1), TOKENS // TOK_DEV)
    routes_turns = jax.random.permutation(jax.random.fold_in(splits[2], 3), TOKENS // TOK_DEV)
    routes = jax.vmap(lambda own, number: assign_block(jax.random.fold_in(splits[2], 2), own, number, TOK_DEV, EXPERTS, 2, CAP, 2))(routes_keys, routes_turns).reshape((TOKENS, 2))
    gate_probs = jnp.clip(0.2 + 0.8 * jax.random.uniform(splits[3], (TOKENS, 2), jnp.float32) ** levels(splits[3], (TOKENS, 2), ((0, 32),), -0.2, 0.2), 0.2, 1.0)
    expert_place = jax.random.permutation(splits[4], EXPERTS).astype(jnp.int32)
    gate_online = noise(splits[5], (UNITS, D, FF_HALF), D ** -0.5, 0.125, ((0, 32),))
    up_online = noise(splits[6], (UNITS, D, FF_HALF), D ** -0.5, 0.125, ((0, 32),))
    down_online = noise(splits[7], (UNITS, FF_HALF, D), FF ** -0.5, 0.25, ((0, 32),))
    gate_target = noise(splits[8], (UNITS, D, FF_HALF), D ** -0.5, 0.125, ((0, 32),))
    up_target = noise(splits[9], (UNITS, D, FF_HALF), D ** -0.5, 0.125, ((0, 32),))
    down_target = noise(splits[10], (UNITS, FF_HALF, D), FF ** -0.5, 0.25, ((0, 32),))
    return dict(x_online=x_online, x_target=x_target, routes=routes, gate_probs=gate_probs, expert_place=expert_place, gate_online=gate_online, up_online=up_online, down_online=down_online, gate_target=gate_target, up_target=up_target, down_target=down_target)


contract_last = (((1,), (1,)), ((), ()))
contract_first = (((0,), (0,)), ((), ()))


def hidden_forward(inputs, w_gate, w_up):
    pre_gate = jnp.dot(inputs, w_gate, preferred_element_type=jnp.float32)
    pre_up = jnp.dot(inputs, w_up, preferred_element_type=jnp.float32)
    hidden = (jax.nn.silu(pre_gate) * pre_up).astype(jnp.bfloat16)
    return pre_gate, pre_up, hidden


def hidden_grads(cotangent, pre_gate, pre_up, w_down):
    d_hidden = lax.dot_general(cotangent, w_down, contract_last, preferred_element_type=jnp.float32)
    sigmoid_gate = jax.nn.sigmoid(pre_gate)
    d_gate = (d_hidden * pre_up * sigmoid_gate * (1.0 + pre_gate * (1.0 - sigmoid_gate))).astype(jnp.bfloat16)
    d_up = (d_hidden * jax.nn.silu(pre_gate)).astype(jnp.bfloat16)
    return d_gate, d_up


def input_rows(d_gate, d_up, w_gate, w_up):
    total = lax.dot_general(d_gate, w_gate, contract_last, preferred_element_type=jnp.float32)
    total = total + lax.dot_general(d_up, w_up, contract_last, preferred_element_type=jnp.float32)
    return total.astype(jnp.bfloat16)


def outer_sum(left, right):
    return lax.dot_general(left, right, contract_first, preferred_element_type=jnp.float32)


def whole_expert(w_gate, w_up, w_down, slot_index):
    pair_gate = lax.dynamic_slice_in_dim(w_gate, 2 * slot_index, 2, 0)
    pair_up = lax.dynamic_slice_in_dim(w_up, 2 * slot_index, 2, 0)
    pair_down = lax.dynamic_slice_in_dim(w_down, 2 * slot_index, 2, 0)
    gate_full = jnp.concatenate([pair_gate[0], pair_gate[1]], axis=1)
    up_full = jnp.concatenate([pair_up[0], pair_up[1]], axis=1)
    down_full = jnp.concatenate([pair_down[0], pair_down[1]], axis=0)
    return gate_full, up_full, down_full


def reference(x_online, x_target, routes, gate_probs, expert_place, gate_online, up_online, down_online, gate_target, up_target, down_target):
    blocks = N_DP * N_EXPERT
    per_expert = blocks * CAP
    assignments = 2 * TOKENS
    chosen = routes.reshape(blocks, 2 * TOK_DEV)
    expert_iota = jnp.arange(EXPERTS, dtype=jnp.int32)
    onehot = (chosen[:, :, None] == expert_iota[None, None, :]).astype(jnp.int32)
    before = jnp.cumsum(onehot, axis=1) - onehot
    position = jnp.sum(before * onehot, axis=2)
    slot_place = expert_place[chosen]
    block_index = jnp.arange(blocks, dtype=jnp.int32)[:, None]
    row_index = (slot_place * per_expert + block_index * CAP + position).reshape(-1).astype(jnp.int32)
    assignment = jnp.arange(assignments, dtype=jnp.int32)
    row_owner = jnp.full((EXPERTS * per_expert,), assignments, jnp.int32).at[row_index].set(assignment)
    filled = row_owner < assignments
    assign_of = jnp.minimum(row_owner, assignments - 1).astype(jnp.int32)
    token_of = (assign_of // 2).astype(jnp.int32)

    def slot_rows(source, index_table, slot_index):
        picked = lax.dynamic_slice_in_dim(index_table, slot_index * per_expert, per_expert)
        present = lax.dynamic_slice_in_dim(filled, slot_index * per_expert, per_expert)
        return jnp.where(present[:, None], source[picked], jnp.zeros((), source.dtype))

    def forward_slot(slot_index):
        inputs_online = slot_rows(x_online, token_of, slot_index)
        inputs_target = slot_rows(x_target, token_of, slot_index)
        gate_full, up_full, down_full = whole_expert(gate_online, up_online, down_online, slot_index)
        hidden = hidden_forward(inputs_online, gate_full, up_full)[2]
        out_online = jnp.dot(hidden, down_full, preferred_element_type=jnp.float32).astype(jnp.bfloat16)
        gate_full, up_full, down_full = whole_expert(gate_target, up_target, down_target, slot_index)
        hidden = hidden_forward(inputs_target, gate_full, up_full)[2]
        out_target = jnp.dot(hidden, down_full, preferred_element_type=jnp.float32).astype(jnp.bfloat16)
        return out_online, out_target

    slots = jnp.arange(EXPERTS, dtype=jnp.int32)
    outs_online, outs_target = lax.map(forward_slot, slots)
    y_online = jnp.sum(outs_online.reshape(-1, D)[row_index].reshape(TOKENS, 2, D).astype(jnp.float32) * gate_probs[:, :, None], axis=1)
    y_target = jnp.sum(outs_target.reshape(-1, D)[row_index].reshape(TOKENS, 2, D).astype(jnp.float32) * gate_probs[:, :, None], axis=1)
    cotangent = (gate_probs[:, :, None] * (y_online - y_target)[:, None, :]).astype(jnp.bfloat16).reshape(assignments, D)

    def backward_slot(slot_index):
        inputs_online = slot_rows(x_online, token_of, slot_index)
        cot_rows = slot_rows(cotangent, assign_of, slot_index)
        gate_full, up_full, down_full = whole_expert(gate_online, up_online, down_online, slot_index)
        pre_gate, pre_up, hidden = hidden_forward(inputs_online, gate_full, up_full)
        d_gate, d_up = hidden_grads(cot_rows, pre_gate, pre_up, down_full)
        d_rows = input_rows(d_gate, d_up, gate_full, up_full)
        g_gate = outer_sum(inputs_online, d_gate).astype(jnp.bfloat16)
        g_up = outer_sum(inputs_online, d_up).astype(jnp.bfloat16)
        g_down = outer_sum(hidden, cot_rows).astype(jnp.bfloat16)
        return d_rows, g_gate, g_up, g_down

    d_all, g_gate, g_up, g_down = lax.map(backward_slot, slots)
    input_grad = jnp.sum(d_all.reshape(-1, D)[row_index].reshape(TOKENS, 2, D).astype(jnp.float32), axis=1).astype(jnp.bfloat16)
    grad_gate = g_gate.reshape(EXPERTS, D, 2, FF_HALF).transpose(0, 2, 1, 3).reshape(UNITS, D, FF_HALF)
    grad_up = g_up.reshape(EXPERTS, D, 2, FF_HALF).transpose(0, 2, 1, 3).reshape(UNITS, D, FF_HALF)
    grad_down = g_down.reshape(UNITS, FF_HALF, D)
    return input_grad, grad_gate, grad_up, grad_down
```

```python
import functools

import jax
import jax.numpy as jnp
from jax import lax
from jax.experimental import pallas as pl
from jax.experimental.pallas import tpu as pltpu
from jax.sharding import PartitionSpec as P

contract_last = (((1,), (1,)), ((), ()))
contract_first = (((0,), (0,)), ((), ()))


def swapped(block, axis, bit):
    count = lax.axis_size(axis)
    route = []
    for low in range(count):
        high = low | 1 << bit
        if high != low and high < count:
            route += [(low, high), (high, low)]
    return lax.ppermute(block, axis, route)


def hidden_forward(inputs, w_gate, w_up):
    pre_gate = jnp.dot(inputs, w_gate, preferred_element_type=jnp.float32)
    pre_up = jnp.dot(inputs, w_up, preferred_element_type=jnp.float32)
    hidden = (jax.nn.silu(pre_gate) * pre_up).astype(jnp.bfloat16)
    return (pre_gate, pre_up, hidden)


def hidden_grads(cotangent, pre_gate, pre_up, w_down):
    d_hidden = lax.dot_general(cotangent, w_down, contract_last, preferred_element_type=jnp.float32)
    sigmoid_gate = jax.nn.sigmoid(pre_gate)
    d_gate = (d_hidden * pre_up * sigmoid_gate * (1.0 + pre_gate * (1.0 - sigmoid_gate))).astype(
        jnp.bfloat16
    )
    d_up = (d_hidden * jax.nn.silu(pre_gate)).astype(jnp.bfloat16)
    return (d_gate, d_up)


def input_rows(d_gate, d_up, w_gate, w_up):
    total = lax.dot_general(d_gate, w_gate, contract_last, preferred_element_type=jnp.float32)
    total = total + lax.dot_general(d_up, w_up, contract_last, preferred_element_type=jnp.float32)
    return total.astype(jnp.bfloat16)


def outer_sum(left, right):
    return lax.dot_general(left, right, contract_first, preferred_element_type=jnp.float32)


def shards_plain(
    x_online,
    x_target,
    routes,
    gate_probs,
    expert_place,
    gate_online,
    up_online,
    down_online,
    gate_target,
    up_target,
    down_target,
):
    tok_rows, model_width = x_online.shape
    dp_count = lax.axis_size("dp")
    expert_count = lax.axis_size("expert")
    unit_count = dp_count * expert_count
    experts = expert_place.shape[0]
    capacity = 2 * ((2 * tok_rows + experts - 1) // experts)
    half_cap = capacity // 2
    half_width = gate_online.shape[2]
    chosen = routes.reshape(-1)
    onehot = (chosen[:, None] == jnp.arange(experts, dtype=jnp.int32)[None, :]).astype(jnp.int32)
    before = jnp.cumsum(onehot, axis=0) - onehot
    position = jnp.sum(before * onehot, axis=1)
    slot_place = jnp.sum(onehot * expert_place[None, :], axis=1)
    flat_slot = (2 * slot_place + position // half_cap) * half_cap + position % half_cap
    owner_token = jnp.arange(2 * tok_rows, dtype=jnp.int32) // 2

    def to_units(source):
        blank_rows = jnp.zeros((unit_count * half_cap, model_width), source.dtype)
        return (
            blank_rows.at[flat_slot]
            .set(source)
            .reshape(dp_count, expert_count, half_cap, model_width)
        )

    def from_units(block):
        picked = block.reshape(unit_count * half_cap, model_width)[flat_slot]
        return picked.astype(jnp.float32).reshape(tok_rows, 2, model_width)

    partner = swapped(
        (gate_online, up_online, down_online, gate_target, up_target, down_target), "expert", 0
    )
    gate_full = jnp.concatenate([gate_online[0], partner[0][0]], axis=1)
    up_full = jnp.concatenate([up_online[0], partner[1][0]], axis=1)
    down_full = jnp.concatenate([down_online[0], partner[2][0]], axis=0)
    gate_tfull = jnp.concatenate([gate_target[0], partner[3][0]], axis=1)
    up_tfull = jnp.concatenate([up_target[0], partner[4][0]], axis=1)
    down_tfull = jnp.concatenate([down_target[0], partner[5][0]], axis=0)
    recv_online, recv_target = (
        lax.all_to_all(
            lax.all_to_all(
                to_units(x_online[owner_token]), "dp", split_axis=0, concat_axis=0, tiled=True
            ),
            "expert",
            split_axis=1,
            concat_axis=1,
            tiled=True,
        ),
        lax.all_to_all(
            lax.all_to_all(
                to_units(x_target[owner_token]), "dp", split_axis=0, concat_axis=0, tiled=True
            ),
            "expert",
            split_axis=1,
            concat_axis=1,
            tiled=True,
        ),
    )
    unit_shape = recv_online.shape
    inputs_online = recv_online.reshape(-1, model_width)
    inputs_target = recv_target.reshape(-1, model_width)
    pre_gate, pre_up, hidden = hidden_forward(inputs_online, gate_full, up_full)
    out_online = jnp.dot(hidden, down_full, preferred_element_type=jnp.float32).astype(jnp.bfloat16)
    hidden_target = hidden_forward(inputs_target, gate_tfull, up_tfull)[2]
    out_target = jnp.dot(hidden_target, down_tfull, preferred_element_type=jnp.float32).astype(
        jnp.bfloat16
    )
    back_online, back_target = (
        lax.all_to_all(
            lax.all_to_all(
                out_online.reshape(unit_shape), "dp", split_axis=0, concat_axis=0, tiled=True
            ),
            "expert",
            split_axis=1,
            concat_axis=1,
            tiled=True,
        ),
        lax.all_to_all(
            lax.all_to_all(
                out_target.reshape(unit_shape), "dp", split_axis=0, concat_axis=0, tiled=True
            ),
            "expert",
            split_axis=1,
            concat_axis=1,
            tiled=True,
        ),
    )
    y_online = jnp.sum(from_units(back_online) * gate_probs[:, :, None], axis=1)
    y_target = jnp.sum(from_units(back_target) * gate_probs[:, :, None], axis=1)
    cotangent = (
        (gate_probs[:, :, None] * (y_online - y_target)[:, None, :])
        .astype(jnp.bfloat16)
        .reshape(2 * tok_rows, model_width)
    )
    cot_recv = lax.all_to_all(
        lax.all_to_all(to_units(cotangent), "dp", split_axis=0, concat_axis=0, tiled=True),
        "expert",
        split_axis=1,
        concat_axis=1,
        tiled=True,
    )
    cot_rows = cot_recv.reshape(-1, model_width)
    d_gate, d_up = hidden_grads(cot_rows, pre_gate, pre_up, down_full)
    d_rows = input_rows(d_gate, d_up, gate_full, up_full)
    back_grads = lax.all_to_all(
        lax.all_to_all(d_rows.reshape(unit_shape), "dp", split_axis=0, concat_axis=0, tiled=True),
        "expert",
        split_axis=1,
        concat_axis=1,
        tiled=True,
    )
    input_grad = jnp.sum(from_units(back_grads), axis=1).astype(jnp.bfloat16)
    g_gate = outer_sum(inputs_online, d_gate)
    g_up = outer_sum(inputs_online, d_up)
    g_down = outer_sum(hidden, cot_rows)
    sent = (
        swapped(g_gate[:, half_width:].astype(jnp.bfloat16), "expert", 0).astype(jnp.float32),
        swapped(g_up[:, half_width:].astype(jnp.bfloat16), "expert", 0).astype(jnp.float32),
        swapped(g_down[half_width:].astype(jnp.bfloat16), "expert", 0).astype(jnp.float32),
    )
    grad_gate = g_gate[:, :half_width] + sent[0]
    grad_up = g_up[:, :half_width] + sent[1]
    grad_down = g_down[:half_width] + sent[2]
    return (
        input_grad,
        grad_gate.astype(jnp.bfloat16)[None],
        grad_up.astype(jnp.bfloat16)[None],
        grad_down.astype(jnp.bfloat16)[None],
    )


MESH = pl.DeviceIdType.MESH
F32 = jnp.float32
BF16 = jnp.bfloat16


def dot(left, right, dims=(((1,), (0,)), ((), ()))):
    return lax.dot_general(left, right, dims, preferred_element_type=F32)


def step_kernel(
    slots,
    n_ex,
    cap,
    flat_ref,
    flat_t_ref,
    probs_ref,
    xo_ref,
    xt_ref,
    w0_ref,
    w1_ref,
    w2_ref,
    w3_ref,
    w4_ref,
    w5_ref,
    ig_ref,
    gg_ref,
    gu_ref,
    gd_ref,
    wg,
    wu,
    wd,
    sx,
    rx,
    pd,
    pr,
    ret,
    rc,
    pre_g,
    pre_u,
    hid,
    dgu,
    w_sem,
    send_sem,
    recv_sem,
    fsend_sem,
    frecv_sem,
    ysend_sem,
    yrecv_sem,
    bsend_sem,
    brecv_sem,
):
    tok, width = xo_ref.shape
    rows = slots * cap
    half = wg.shape[2]
    tile = 512
    dp, ex = lax.axis_index("dp"), lax.axis_index("expert")
    side = lax.rem(ex, 2)
    me = lax.div(dp * n_ex + ex, 2)
    partner = (dp, ex + 1 - 2 * side)

    def peer(slot):
        unit = 2 * slot + side
        return (lax.div(unit, n_ex), lax.rem(unit, n_ex))

    def chunk(index):
        return pl.ds(pl.multiple_of(index * cap, cap), cap)

    barrier = pltpu.get_barrier_semaphore()

    def greet(o, carry):
        pl.semaphore_signal(
            barrier, inc=1, device_id=peer(lax.rem(me + o, slots)), device_id_type=MESH
        )
        return carry

    lax.fori_loop(1, slots, greet, 0)
    pl.semaphore_signal(barrier, inc=1, device_id=partner, device_id_type=MESH)

    weight_copies = [
        pltpu.make_async_copy(source, target, w_sem.at[i])
        for i, (source, target) in enumerate(
            [
                (w0_ref, wg.at[0]),
                (w1_ref, wu.at[0]),
                (w2_ref, wd.at[0]),
                (w3_ref, wg.at[1]),
                (w4_ref, wu.at[1]),
                (w5_ref, wd.at[1]),
            ]
        )
    ]
    for copy in weight_copies:
        copy.start()

    def one_hot(compare):
        return jnp.where(compare, 1.0, 0.0).astype(BF16)

    row_iota = lax.broadcasted_iota(jnp.int32, (rows, tok), 0)
    put = [one_hot(row_iota == flat_t_ref[k : k + 1, :]) for k in range(2)]
    put_any = one_hot((row_iota == flat_t_ref[0:1, :]) | (row_iota == flat_t_ref[1:2, :]))
    col_iota = lax.broadcasted_iota(jnp.int32, (tok, rows), 1)
    take = [one_hot(col_iota == flat_ref[:, k : k + 1]) for k in range(2)]
    take_any = one_hot((col_iota == flat_ref[:, 0:1]) | (col_iota == flat_ref[:, 1:2]))

    def columns(body):
        def step(i, carry):
            body(pl.ds(pl.multiple_of(i * tile, tile), tile))
            return carry

        lax.fori_loop(0, width // tile, step, 0)

    def each(low, body):
        def step(o, carry):
            body(o)
            return carry

        lax.fori_loop(low, slots, step, 0)

    def out_copy(net, dst, o):
        to = lax.rem(me + o, slots)
        return pltpu.make_async_remote_copy(
            src_ref=sx.at[net, chunk(to)],
            dst_ref=dst.at[0, chunk(o)],
            send_sem=send_sem.at[net, o],
            recv_sem=recv_sem.at[net, o],
            device_id=peer(to),
            device_id_type=MESH,
        )

    def fwd_copy(net, dst, o):
        return pltpu.make_async_remote_copy(
            src_ref=dst.at[0, chunk(o)],
            dst_ref=dst.at[1, chunk(o)],
            send_sem=fsend_sem.at[net, o],
            recv_sem=frecv_sem.at[net, o],
            device_id=partner,
            device_id_type=MESH,
        )

    def scatter_start(net, dst):
        each(1, lambda o: out_copy(net, dst, o).start())
        dst[0, 0:cap] = sx[net, chunk(me)]
        fwd_copy(net, dst, 0).start()

    def relay(net, dst):
        def body(o):
            out_copy(net, dst, o).wait_recv()
            fwd_copy(net, dst, o).start()

        each(1, body)

    def arrived(net, dst):
        each(0, lambda o: fwd_copy(net, dst, o).wait_recv())

    def scatter_end(net, dst):
        each(0, lambda o: fwd_copy(net, dst, o).wait_send())
        each(1, lambda o: out_copy(net, dst, o).wait_send())

    def pair_copy(turn, o):
        return pltpu.make_async_remote_copy(
            src_ref=pd.at[1, chunk(o)],
            dst_ref=pr.at[turn, chunk(o)],
            send_sem=ysend_sem.at[turn, o],
            recv_sem=yrecv_sem.at[turn, o],
            device_id=partner,
            device_id_type=MESH,
        )

    def back_copy(turn, o):
        return pltpu.make_async_remote_copy(
            src_ref=pd.at[0, chunk(o)],
            dst_ref=ret.at[turn, chunk(me)],
            send_sem=bsend_sem.at[turn, o],
            recv_sem=brecv_sem.at[turn, o],
            device_id=peer(lax.rem(me - o + slots, slots)),
            device_id_type=MESH,
        )

    def add_part(turn, o):
        pair_copy(turn, o).wait_recv()
        total = pd[0, chunk(o)].astype(F32) + pr[turn, chunk(o)].astype(F32)
        return total.astype(BF16)

    def give_back(turn):
        def body(o):
            pd[0, chunk(o)] = add_part(turn, o)
            back_copy(turn, o).start()

        each(1, body)
        ret[turn, chunk(me)] = add_part(turn, 0)

    def back_end(turn):
        each(0, lambda o: pair_copy(turn, o).wait_send())
        each(1, lambda o: back_copy(turn, o).wait_send())
        each(1, lambda o: back_copy(turn, o).wait_recv())

    def place_online(cols):
        sx[0, :, cols] = dot(put_any, xo_ref[:, cols]).astype(BF16)

    def place_target(cols):
        sx[1, :, cols] = dot(put_any, xt_ref[:, cols]).astype(BF16)

    columns(place_online)
    pl.semaphore_wait(barrier, slots)
    scatter_start(0, rx.at[0])
    columns(place_target)
    scatter_start(1, rx.at[1])
    for copy in weight_copies:
        copy.wait()
    relay(0, rx.at[0])
    relay(1, rx.at[1])

    def forward(net, part):
        gate = dot(rx[net, part], wg[net])
        up = dot(rx[net, part], wu[net])
        hid[net, part] = (gate * jax.nn.sigmoid(gate) * up).astype(BF16)
        if net == 0:
            pre_g[part] = gate
            pre_u[part] = up

    forward(0, 0)
    arrived(0, rx.at[0])
    forward(0, 1)
    forward(1, 0)
    arrived(1, rx.at[1])
    forward(1, 1)

    for part in (1, 0):

        def outputs(cols, part=part):
            diff = dot(hid[0, part], wd[0, :, cols]) - dot(hid[1, part], wd[1, :, cols])
            pd[part, :, cols] = diff.astype(BF16)

        columns(outputs)
        if part == 1:
            each(0, lambda o: pair_copy(0, o).start())
    give_back(0)
    scatter_end(0, rx.at[0])
    scatter_end(1, rx.at[1])
    back_end(0)

    p0, p1 = probs_ref[:, 0:1], probs_ref[:, 1:2]

    def cotangents(cols):
        back = ret[0, :, cols]
        diff = p0 * dot(take[0], back) + p1 * dot(take[1], back)
        cot0, cot1 = (p0 * diff).astype(BF16), (p1 * diff).astype(BF16)
        sx[2, :, cols] = (dot(put[0], cot0) + dot(put[1], cot1)).astype(BF16)

    columns(cotangents)
    scatter_start(2, rc)
    relay(2, rc)

    def hidden_back(part):
        d_hidden = dot(rc[part], wd[0], contract_last)
        gate, up = pre_g[part], pre_u[part]
        sig = jax.nn.sigmoid(gate)
        dgu[0, part] = (d_hidden * up * sig * (1.0 + gate * (1.0 - sig))).astype(BF16)
        dgu[1, part] = (d_hidden * (gate * sig)).astype(BF16)

    hidden_back(0)
    arrived(2, rc)
    hidden_back(1)
    for part in (1, 0):

        def row_grads(cols, part=part):
            total = dot(dgu[0, part], wg[0, cols, :], contract_last)
            total = total + dot(dgu[1, part], wu[0, cols, :], contract_last)
            pd[part, :, cols] = total.astype(BF16)

        columns(row_grads)
        if part == 1:
            each(0, lambda o: pair_copy(1, o).start())
    give_back(1)

    def weight_grads(cols):
        for index, target in ((0, gg_ref), (1, gu_ref)):
            total = dot(rx[0, 0, :, cols], dgu[index, 0], contract_first)
            total = total + dot(rx[0, 1, :, cols], dgu[index, 1], contract_first)
            target[cols, :] = total.astype(BF16)
        total = dot(hid[0, 0], rc[0, :, cols], contract_first)
        total = total + dot(hid[0, 1], rc[1, :, cols], contract_first)
        gd_ref[:, cols] = total.astype(BF16)

    columns(weight_grads)
    scatter_end(2, rc)
    back_end(1)

    def inputs_grad(cols):
        ig_ref[:, cols] = dot(take_any, ret[1, :, cols]).astype(BF16)

    columns(inputs_grad)


def shards(
    x_online,
    x_target,
    routes,
    gate_probs,
    expert_place,
    gate_online,
    up_online,
    down_online,
    gate_target,
    up_target,
    down_target,
):
    tok, width = x_online.shape
    slots = expert_place.shape[0]
    n_ex = lax.axis_size("expert")
    cap = 2 * ((2 * tok + slots - 1) // slots)
    rows = slots * cap
    half = gate_online.shape[2]
    if cap % 16 or 2 * slots != lax.axis_size("dp") * n_ex:
        return shards_plain(
            x_online,
            x_target,
            routes,
            gate_probs,
            expert_place,
            gate_online,
            up_online,
            down_online,
            gate_target,
            up_target,
            down_target,
        )
    chosen = routes.reshape(-1)
    onehot = (chosen[:, None] == jnp.arange(slots, dtype=jnp.int32)[None, :]).astype(jnp.int32)
    before = jnp.cumsum(onehot, axis=0) - onehot
    flat = jnp.sum((before + cap * expert_place[None, :]) * onehot, axis=1).reshape(tok, 2)
    vmem = pl.BlockSpec(memory_space=pltpu.VMEM)
    hbm = pl.BlockSpec(memory_space=pl.ANY)
    dma = pltpu.SemaphoreType.DMA
    outs = pl.pallas_call(
        functools.partial(step_kernel, slots, n_ex, cap),
        out_shape=(
            jax.ShapeDtypeStruct((tok, width), BF16),
            jax.ShapeDtypeStruct((width, half), BF16),
            jax.ShapeDtypeStruct((width, half), BF16),
            jax.ShapeDtypeStruct((half, width), BF16),
        ),
        in_specs=[vmem] * 5 + [hbm] * 6,
        out_specs=(vmem,) * 4,
        scratch_shapes=[
            pltpu.VMEM((2, width, half), BF16),
            pltpu.VMEM((2, width, half), BF16),
            pltpu.VMEM((2, half, width), BF16),
            pltpu.VMEM((3, rows, width), BF16),
            pltpu.VMEM((2, 2, rows, width), BF16),
            pltpu.VMEM((2, rows, width), BF16),
            pltpu.VMEM((2, rows, width), BF16),
            pltpu.VMEM((2, rows, width), BF16),
            pltpu.VMEM((2, rows, width), BF16),
            pltpu.VMEM((2, rows, half), F32),
            pltpu.VMEM((2, rows, half), F32),
            pltpu.VMEM((2, 2, rows, half), BF16),
            pltpu.VMEM((2, 2, rows, half), BF16),
            dma((6,)),
            dma((3, slots)),
            dma((3, slots)),
            dma((3, slots)),
            dma((3, slots)),
            dma((2, slots)),
            dma((2, slots)),
            dma((2, slots)),
            dma((2, slots)),
        ],
        compiler_params=pltpu.CompilerParams(
            collective_id=0, has_side_effects=True, vmem_limit_bytes=60 * 2**20
        ),
    )(
        flat,
        flat.T,
        gate_probs,
        x_online,
        x_target,
        gate_online[0],
        up_online[0],
        down_online[0],
        gate_target[0],
        up_target[0],
        down_target[0],
    )
    return (outs[0], outs[1][None], outs[2][None], outs[3][None])


def solution(mesh):
    in_specs = (
        P(("dp", "expert"), None),
        P(("dp", "expert"), None),
        P(("dp", "expert"), None),
        P(("dp", "expert"), None),
        P(),
        P(("dp", "expert"), None, None),
        P(("dp", "expert"), None, None),
        P(("dp", "expert"), None, None),
        P(("dp", "expert"), None, None),
        P(("dp", "expert"), None, None),
        P(("dp", "expert"), None, None),
    )
    out_specs = (
        P(("dp", "expert"), None),
        P(("dp", "expert"), None, None),
        P(("dp", "expert"), None, None),
        P(("dp", "expert"), None, None),
    )
    return jax.shard_map(shards, mesh=mesh, in_specs=in_specs, out_specs=out_specs, check_vma=False)
```

```python
import functools

import jax
import jax.numpy as jnp
from jax import lax
from jax.experimental import pallas as pl
from jax.experimental.pallas import tpu as pltpu
from jax.sharding import PartitionSpec as P

contract_last = (((1,), (1,)), ((), ()))
contract_first = (((0,), (0,)), ((), ()))


def swapped(block, axis, bit):
    count = lax.axis_size(axis)
    route = []
    for low in range(count):
        high = low | 1 << bit
        if high != low and high < count:
            route += [(low, high), (high, low)]
    return lax.ppermute(block, axis, route)


def hidden_forward(inputs, w_gate, w_up):
    pre_gate = jnp.dot(inputs, w_gate, preferred_element_type=jnp.float32)
    pre_up = jnp.dot(inputs, w_up, preferred_element_type=jnp.float32)
    hidden = (jax.nn.silu(pre_gate) * pre_up).astype(jnp.bfloat16)
    return (pre_gate, pre_up, hidden)


def hidden_grads(cotangent, pre_gate, pre_up, w_down):
    d_hidden = lax.dot_general(cotangent, w_down, contract_last, preferred_element_type=jnp.float32)
    sigmoid_gate = jax.nn.sigmoid(pre_gate)
    d_gate = (d_hidden * pre_up * sigmoid_gate * (1.0 + pre_gate * (1.0 - sigmoid_gate))).astype(
        jnp.bfloat16
    )
    d_up = (d_hidden * jax.nn.silu(pre_gate)).astype(jnp.bfloat16)
    return (d_gate, d_up)


def input_rows(d_gate, d_up, w_gate, w_up):
    total = lax.dot_general(d_gate, w_gate, contract_last, preferred_element_type=jnp.float32)
    total = total + lax.dot_general(d_up, w_up, contract_last, preferred_element_type=jnp.float32)
    return total.astype(jnp.bfloat16)


def outer_sum(left, right):
    return lax.dot_general(left, right, contract_first, preferred_element_type=jnp.float32)


def shards_plain(
    x_online,
    x_target,
    routes,
    gate_probs,
    expert_place,
    gate_online,
    up_online,
    down_online,
    gate_target,
    up_target,
    down_target,
):
    tok_rows, model_width = x_online.shape
    dp_count = lax.axis_size("dp")
    expert_count = lax.axis_size("expert")
    unit_count = dp_count * expert_count
    experts = expert_place.shape[0]
    capacity = 2 * ((2 * tok_rows + experts - 1) // experts)
    half_cap = capacity // 2
    half_width = gate_online.shape[2]
    chosen = routes.reshape(-1)
    onehot = (chosen[:, None] == jnp.arange(experts, dtype=jnp.int32)[None, :]).astype(jnp.int32)
    before = jnp.cumsum(onehot, axis=0) - onehot
    position = jnp.sum(before * onehot, axis=1)
    slot_place = jnp.sum(onehot * expert_place[None, :], axis=1)
    flat_slot = (2 * slot_place + position // half_cap) * half_cap + position % half_cap
    owner_token = jnp.arange(2 * tok_rows, dtype=jnp.int32) // 2

    def to_units(source):
        blank_rows = jnp.zeros((unit_count * half_cap, model_width), source.dtype)
        return (
            blank_rows.at[flat_slot]
            .set(source)
            .reshape(dp_count, expert_count, half_cap, model_width)
        )

    def from_units(block):
        picked = block.reshape(unit_count * half_cap, model_width)[flat_slot]
        return picked.astype(jnp.float32).reshape(tok_rows, 2, model_width)

    partner = swapped(
        (gate_online, up_online, down_online, gate_target, up_target, down_target), "expert", 0
    )
    gate_full = jnp.concatenate([gate_online[0], partner[0][0]], axis=1)
    up_full = jnp.concatenate([up_online[0], partner[1][0]], axis=1)
    down_full = jnp.concatenate([down_online[0], partner[2][0]], axis=0)
    gate_tfull = jnp.concatenate([gate_target[0], partner[3][0]], axis=1)
    up_tfull = jnp.concatenate([up_target[0], partner[4][0]], axis=1)
    down_tfull = jnp.concatenate([down_target[0], partner[5][0]], axis=0)
    recv_online, recv_target = (
        lax.all_to_all(
            lax.all_to_all(
                to_units(x_online[owner_token]), "dp", split_axis=0, concat_axis=0, tiled=True
            ),
            "expert",
            split_axis=1,
            concat_axis=1,
            tiled=True,
        ),
        lax.all_to_all(
            lax.all_to_all(
                to_units(x_target[owner_token]), "dp", split_axis=0, concat_axis=0, tiled=True
            ),
            "expert",
            split_axis=1,
            concat_axis=1,
            tiled=True,
        ),
    )
    unit_shape = recv_online.shape
    inputs_online = recv_online.reshape(-1, model_width)
    inputs_target = recv_target.reshape(-1, model_width)
    pre_gate, pre_up, hidden = hidden_forward(inputs_online, gate_full, up_full)
    out_online = jnp.dot(hidden, down_full, preferred_element_type=jnp.float32).astype(jnp.bfloat16)
    hidden_target = hidden_forward(inputs_target, gate_tfull, up_tfull)[2]
    out_target = jnp.dot(hidden_target, down_tfull, preferred_element_type=jnp.float32).astype(
        jnp.bfloat16
    )
    back_online, back_target = (
        lax.all_to_all(
            lax.all_to_all(
                out_online.reshape(unit_shape), "dp", split_axis=0, concat_axis=0, tiled=True
            ),
            "expert",
            split_axis=1,
            concat_axis=1,
            tiled=True,
        ),
        lax.all_to_all(
            lax.all_to_all(
                out_target.reshape(unit_shape), "dp", split_axis=0, concat_axis=0, tiled=True
            ),
            "expert",
            split_axis=1,
            concat_axis=1,
            tiled=True,
        ),
    )
    y_online = jnp.sum(from_units(back_online) * gate_probs[:, :, None], axis=1)
    y_target = jnp.sum(from_units(back_target) * gate_probs[:, :, None], axis=1)
    cotangent = (
        (gate_probs[:, :, None] * (y_online - y_target)[:, None, :])
        .astype(jnp.bfloat16)
        .reshape(2 * tok_rows, model_width)
    )
    cot_recv = lax.all_to_all(
        lax.all_to_all(to_units(cotangent), "dp", split_axis=0, concat_axis=0, tiled=True),
        "expert",
        split_axis=1,
        concat_axis=1,
        tiled=True,
    )
    cot_rows = cot_recv.reshape(-1, model_width)
    d_gate, d_up = hidden_grads(cot_rows, pre_gate, pre_up, down_full)
    d_rows = input_rows(d_gate, d_up, gate_full, up_full)
    back_grads = lax.all_to_all(
        lax.all_to_all(d_rows.reshape(unit_shape), "dp", split_axis=0, concat_axis=0, tiled=True),
        "expert",
        split_axis=1,
        concat_axis=1,
        tiled=True,
    )
    input_grad = jnp.sum(from_units(back_grads), axis=1).astype(jnp.bfloat16)
    g_gate = outer_sum(inputs_online, d_gate)
    g_up = outer_sum(inputs_online, d_up)
    g_down = outer_sum(hidden, cot_rows)
    sent = (
        swapped(g_gate[:, half_width:].astype(jnp.bfloat16), "expert", 0).astype(jnp.float32),
        swapped(g_up[:, half_width:].astype(jnp.bfloat16), "expert", 0).astype(jnp.float32),
        swapped(g_down[half_width:].astype(jnp.bfloat16), "expert", 0).astype(jnp.float32),
    )
    grad_gate = g_gate[:, :half_width] + sent[0]
    grad_up = g_up[:, :half_width] + sent[1]
    grad_down = g_down[:half_width] + sent[2]
    return (
        input_grad,
        grad_gate.astype(jnp.bfloat16)[None],
        grad_up.astype(jnp.bfloat16)[None],
        grad_down.astype(jnp.bfloat16)[None],
    )


MESH = pl.DeviceIdType.MESH
F32 = jnp.float32
BF16 = jnp.bfloat16


def dot(left, right, dims=(((1,), (0,)), ((), ()))):
    return lax.dot_general(left, right, dims, preferred_element_type=F32)


def step_kernel(
    slots,
    n_ex,
    cap,
    flat_ref,
    flat_t_ref,
    probs_ref,
    xo_ref,
    xt_ref,
    w0_ref,
    w1_ref,
    w2_ref,
    w3_ref,
    w4_ref,
    w5_ref,
    ig_ref,
    gg_ref,
    gu_ref,
    gd_ref,
    wg,
    wu,
    wd,
    sx,
    rx,
    pd,
    pr,
    ret,
    rc,
    pre_g,
    pre_u,
    hid,
    dgu,
    w_sem,
    send_sem,
    recv_sem,
    fsend_sem,
    frecv_sem,
    ysend_sem,
    yrecv_sem,
    bsend_sem,
    brecv_sem,
):
    tok, width = xo_ref.shape
    rows = slots * cap
    half = wg.shape[2]
    tile = 512
    dp, ex = lax.axis_index("dp"), lax.axis_index("expert")
    side = lax.rem(ex, 2)
    me = lax.div(dp * n_ex + ex, 2)
    partner = (dp, ex + 1 - 2 * side)

    planes = n_ex // 2
    group = slots // planes
    near, window = slots // 2, 3

    def other(i):
        mask = lax.rem(i, group) * planes + lax.div(i, group)
        slot, power = 0, 1
        while power < slots:
            bit = lax.rem(lax.rem(lax.div(me, power), 2) + lax.rem(lax.div(mask, power), 2), 2)
            slot, power = slot + bit * power, 2 * power
        return slot

    def peer(slot):
        unit = 2 * slot + side
        return (lax.div(unit, n_ex), lax.rem(unit, n_ex))

    def chunk(index):
        return pl.ds(pl.multiple_of(index * cap, cap), cap)

    barrier = pltpu.get_barrier_semaphore()

    def greet(o, carry):
        pl.semaphore_signal(
            barrier, inc=1, device_id=peer(other(o)), device_id_type=MESH
        )
        return carry

    lax.fori_loop(1, slots, greet, 0)
    pl.semaphore_signal(barrier, inc=1, device_id=partner, device_id_type=MESH)

    weight_copies = [
        pltpu.make_async_copy(source, target, w_sem.at[i])
        for i, (source, target) in enumerate(
            [
                (w0_ref, wg.at[0]),
                (w1_ref, wu.at[0]),
                (w2_ref, wd.at[0]),
                (w3_ref, wg.at[1]),
                (w4_ref, wu.at[1]),
                (w5_ref, wd.at[1]),
            ]
        )
    ]
    for copy in weight_copies:
        copy.start()

    def one_hot(compare):
        return jnp.where(compare, 1.0, 0.0).astype(BF16)

    row_iota = lax.broadcasted_iota(jnp.int32, (rows, tok), 0)
    put = [one_hot(row_iota == flat_t_ref[k : k + 1, :]) for k in range(2)]
    put_any = one_hot((row_iota == flat_t_ref[0:1, :]) | (row_iota == flat_t_ref[1:2, :]))
    col_iota = lax.broadcasted_iota(jnp.int32, (tok, rows), 1)
    take = [one_hot(col_iota == flat_ref[:, k : k + 1]) for k in range(2)]
    take_any = one_hot((col_iota == flat_ref[:, 0:1]) | (col_iota == flat_ref[:, 1:2]))

    def columns(body):
        def step(i, carry):
            body(pl.ds(pl.multiple_of(i * tile, tile), tile))
            return carry

        lax.fori_loop(0, width // tile, step, 0)

    def each(low, body, high=slots):
        def step(o, carry):
            body(o)
            return carry

        lax.fori_loop(low, high, step, 0)

    def each_down(low, body):
        each(0, lambda o: body(slots - 1 - o), slots - low)

    def out_copy(net, dst, o):
        to = other(o)
        return pltpu.make_async_remote_copy(
            src_ref=sx.at[net, chunk(to)],
            dst_ref=dst.at[0, chunk(o)],
            send_sem=send_sem.at[net, o],
            recv_sem=recv_sem.at[net, o],
            device_id=peer(to),
            device_id_type=MESH,
        )

    def fwd_copy(net, dst, o):
        return pltpu.make_async_remote_copy(
            src_ref=dst.at[0, chunk(o)],
            dst_ref=dst.at[1, chunk(o)],
            send_sem=fsend_sem.at[net, o],
            recv_sem=frecv_sem.at[net, o],
            device_id=partner,
            device_id_type=MESH,
        )

    def start_near(net, dst):
        each(1, lambda o: out_copy(net, dst, o).start(), near)
        dst[0, 0:cap] = sx[net, chunk(me)]
        fwd_copy(net, dst, 0).start()

    def start_far(net, dst):
        each(near, lambda o: out_copy(net, dst, o).start(), near + window)

    def relay(net, dst, then=None):
        def pass_on(o):
            out_copy(net, dst, o).wait_recv()
            fwd_copy(net, dst, o).start()

        def far(o):
            pass_on(o)
            out_copy(net, dst, o).wait_send()
            out_copy(net, dst, o + window).start()

        def last(o):
            pass_on(o)
            out_copy(net, dst, o).wait_send()
            if then is not None:
                out_copy(*then, o - (slots - window - near)).start()

        each(1, pass_on, near)
        if then is not None:
            start_near(*then)
        each(near, far, slots - window)
        each(slots - window, last)

    def arrived(net, dst):
        each(0, lambda o: fwd_copy(net, dst, o).wait_recv())

    def scatter_end(net, dst):
        each(0, lambda o: fwd_copy(net, dst, o).wait_send())
        each(1, lambda o: out_copy(net, dst, o).wait_send(), near)

    def pair_copy(turn, o):
        return pltpu.make_async_remote_copy(
            src_ref=pd.at[1, chunk(o)],
            dst_ref=pr.at[turn, chunk(o)],
            send_sem=ysend_sem.at[turn, o],
            recv_sem=yrecv_sem.at[turn, o],
            device_id=partner,
            device_id_type=MESH,
        )

    def back_copy(turn, o):
        return pltpu.make_async_remote_copy(
            src_ref=pd.at[0, chunk(o)],
            dst_ref=ret.at[turn, chunk(me)],
            send_sem=bsend_sem.at[turn, o],
            recv_sem=brecv_sem.at[turn, o],
            device_id=peer(other(o)),
            device_id_type=MESH,
        )

    def add_part(turn, o):
        pair_copy(turn, o).wait_recv()
        total = pd[0, chunk(o)].astype(F32) + pr[turn, chunk(o)].astype(F32)
        return total.astype(BF16)

    def give_back(turn):
        def body(o):
            pd[0, chunk(o)] = add_part(turn, o)
            back_copy(turn, o).start()

        each_down(1, body)
        ret[turn, chunk(me)] = add_part(turn, 0)

    def back_end(turn):
        each(0, lambda o: pair_copy(turn, o).wait_send())
        each(1, lambda o: back_copy(turn, o).wait_send())
        each(1, lambda o: back_copy(turn, o).wait_recv())

    def place_online(cols):
        sx[0, :, cols] = dot(put_any, xo_ref[:, cols]).astype(BF16)

    def place_target(cols):
        sx[1, :, cols] = dot(put_any, xt_ref[:, cols]).astype(BF16)

    columns(place_online)
    pl.semaphore_wait(barrier, slots)
    start_far(0, rx.at[0])
    start_near(0, rx.at[0])
    columns(place_target)
    for copy in weight_copies:
        copy.wait()
    relay(0, rx.at[0], (1, rx.at[1]))
    relay(1, rx.at[1])

    def forward(net, part):
        gate = dot(rx[net, part], wg[net])
        up = dot(rx[net, part], wu[net])
        hid[net, part] = (gate * jax.nn.sigmoid(gate) * up).astype(BF16)
        if net == 0:
            pre_g[part] = gate
            pre_u[part] = up

    forward(0, 0)
    arrived(0, rx.at[0])
    forward(0, 1)
    forward(1, 0)
    arrived(1, rx.at[1])
    forward(1, 1)

    for part in (1, 0):

        def outputs(cols, part=part):
            diff = dot(hid[0, part], wd[0, :, cols]) - dot(hid[1, part], wd[1, :, cols])
            pd[part, :, cols] = diff.astype(BF16)

        columns(outputs)
        if part == 1:
            each_down(0, lambda o: pair_copy(0, o).start())
    give_back(0)
    scatter_end(0, rx.at[0])
    scatter_end(1, rx.at[1])
    back_end(0)

    p0, p1 = probs_ref[:, 0:1], probs_ref[:, 1:2]

    def cotangents(cols):
        back = ret[0, :, cols]
        diff = p0 * dot(take[0], back) + p1 * dot(take[1], back)
        cot0, cot1 = (p0 * diff).astype(BF16), (p1 * diff).astype(BF16)
        sx[2, :, cols] = (dot(put[0], cot0) + dot(put[1], cot1)).astype(BF16)

    columns(cotangents)
    start_far(2, rc)
    start_near(2, rc)
    relay(2, rc)

    def hidden_back(part):
        d_hidden = dot(rc[part], wd[0], contract_last)
        gate, up = pre_g[part], pre_u[part]
        sig = jax.nn.sigmoid(gate)
        dgu[0, part] = (d_hidden * up * sig * (1.0 + gate * (1.0 - sig))).astype(BF16)
        dgu[1, part] = (d_hidden * (gate * sig)).astype(BF16)

    hidden_back(0)
    arrived(2, rc)
    hidden_back(1)
    for part in (1, 0):

        def row_grads(cols, part=part):
            total = dot(dgu[0, part], wg[0, cols, :], contract_last)
            total = total + dot(dgu[1, part], wu[0, cols, :], contract_last)
            pd[part, :, cols] = total.astype(BF16)

        columns(row_grads)
        if part == 1:
            each_down(0, lambda o: pair_copy(1, o).start())
    give_back(1)

    def weight_grads(cols):
        for index, target in ((0, gg_ref), (1, gu_ref)):
            total = dot(rx[0, 0, :, cols], dgu[index, 0], contract_first)
            total = total + dot(rx[0, 1, :, cols], dgu[index, 1], contract_first)
            target[cols, :] = total.astype(BF16)
        total = dot(hid[0, 0], rc[0, :, cols], contract_first)
        total = total + dot(hid[0, 1], rc[1, :, cols], contract_first)
        gd_ref[:, cols] = total.astype(BF16)

    columns(weight_grads)
    scatter_end(2, rc)
    back_end(1)

    def inputs_grad(cols):
        ig_ref[:, cols] = dot(take_any, ret[1, :, cols]).astype(BF16)

    columns(inputs_grad)


def shards(
    x_online,
    x_target,
    routes,
    gate_probs,
    expert_place,
    gate_online,
    up_online,
    down_online,
    gate_target,
    up_target,
    down_target,
):
    tok, width = x_online.shape
    slots = expert_place.shape[0]
    n_ex = lax.axis_size("expert")
    cap = 2 * ((2 * tok + slots - 1) // slots)
    rows = slots * cap
    half = gate_online.shape[2]
    paired = 2 * slots == lax.axis_size("dp") * n_ex and n_ex % 2 == 0
    halving = slots & (slots - 1) == 0 and n_ex & (n_ex - 1) == 0
    if cap % 16 or slots < 8 or not (paired and halving):
        return shards_plain(
            x_online,
            x_target,
            routes,
            gate_probs,
            expert_place,
            gate_online,
            up_online,
            down_online,
            gate_target,
            up_target,
            down_target,
        )
    chosen = routes.reshape(-1)
    onehot = (chosen[:, None] == jnp.arange(slots, dtype=jnp.int32)[None, :]).astype(jnp.int32)
    before = jnp.cumsum(onehot, axis=0) - onehot
    flat = jnp.sum((before + cap * expert_place[None, :]) * onehot, axis=1).reshape(tok, 2)
    vmem = pl.BlockSpec(memory_space=pltpu.VMEM)
    hbm = pl.BlockSpec(memory_space=pl.ANY)
    dma = pltpu.SemaphoreType.DMA
    outs = pl.pallas_call(
        functools.partial(step_kernel, slots, n_ex, cap),
        out_shape=(
            jax.ShapeDtypeStruct((tok, width), BF16),
            jax.ShapeDtypeStruct((width, half), BF16),
            jax.ShapeDtypeStruct((width, half), BF16),
            jax.ShapeDtypeStruct((half, width), BF16),
        ),
        in_specs=[vmem] * 5 + [hbm] * 6,
        out_specs=(vmem,) * 4,
        scratch_shapes=[
            pltpu.VMEM((2, width, half), BF16),
            pltpu.VMEM((2, width, half), BF16),
            pltpu.VMEM((2, half, width), BF16),
            pltpu.VMEM((3, rows, width), BF16),
            pltpu.VMEM((2, 2, rows, width), BF16),
            pltpu.VMEM((2, rows, width), BF16),
            pltpu.VMEM((2, rows, width), BF16),
            pltpu.VMEM((2, rows, width), BF16),
            pltpu.VMEM((2, rows, width), BF16),
            pltpu.VMEM((2, rows, half), F32),
            pltpu.VMEM((2, rows, half), F32),
            pltpu.VMEM((2, 2, rows, half), BF16),
            pltpu.VMEM((2, 2, rows, half), BF16),
            dma((6,)),
            dma((3, slots)),
            dma((3, slots)),
            dma((3, slots)),
            dma((3, slots)),
            dma((2, slots)),
            dma((2, slots)),
            dma((2, slots)),
            dma((2, slots)),
        ],
        compiler_params=pltpu.CompilerParams(
            collective_id=0, has_side_effects=True, vmem_limit_bytes=60 * 2**20
        ),
    )(
        flat,
        flat.T,
        gate_probs,
        x_online,
        x_target,
        gate_online[0],
        up_online[0],
        down_online[0],
        gate_target[0],
        up_target[0],
        down_target[0],
    )
    return (outs[0], outs[1][None], outs[2][None], outs[3][None])


def solution(mesh):
    in_specs = (
        P(("dp", "expert"), None),
        P(("dp", "expert"), None),
        P(("dp", "expert"), None),
        P(("dp", "expert"), None),
        P(),
        P(("dp", "expert"), None, None),
        P(("dp", "expert"), None, None),
        P(("dp", "expert"), None, None),
        P(("dp", "expert"), None, None),
        P(("dp", "expert"), None, None),
        P(("dp", "expert"), None, None),
    )
    out_specs = (
        P(("dp", "expert"), None),
        P(("dp", "expert"), None, None),
        P(("dp", "expert"), None, None),
        P(("dp", "expert"), None, None),
    )
    return jax.shard_map(shards, mesh=mesh, in_specs=in_specs, out_specs=out_specs, check_vma=False)
```

```python
import functools

import jax
import jax.numpy as jnp
from jax import lax
from jax.experimental import pallas as pl
from jax.experimental.pallas import tpu as pltpu
from jax.sharding import PartitionSpec as P

contract_last = (((1,), (1,)), ((), ()))
contract_first = (((0,), (0,)), ((), ()))


def swapped(block, axis, bit):
    count = lax.axis_size(axis)
    route = []
    for low in range(count):
        high = low | 1 << bit
        if high != low and high < count:
            route += [(low, high), (high, low)]
    return lax.ppermute(block, axis, route)


def hidden_forward(inputs, w_gate, w_up):
    pre_gate = jnp.dot(inputs, w_gate, preferred_element_type=jnp.float32)
    pre_up = jnp.dot(inputs, w_up, preferred_element_type=jnp.float32)
    hidden = (jax.nn.silu(pre_gate) * pre_up).astype(jnp.bfloat16)
    return (pre_gate, pre_up, hidden)


def hidden_grads(cotangent, pre_gate, pre_up, w_down):
    d_hidden = lax.dot_general(cotangent, w_down, contract_last, preferred_element_type=jnp.float32)
    sigmoid_gate = jax.nn.sigmoid(pre_gate)
    d_gate = (d_hidden * pre_up * sigmoid_gate * (1.0 + pre_gate * (1.0 - sigmoid_gate))).astype(
        jnp.bfloat16
    )
    d_up = (d_hidden * jax.nn.silu(pre_gate)).astype(jnp.bfloat16)
    return (d_gate, d_up)


def input_rows(d_gate, d_up, w_gate, w_up):
    total = lax.dot_general(d_gate, w_gate, contract_last, preferred_element_type=jnp.float32)
    total = total + lax.dot_general(d_up, w_up, contract_last, preferred_element_type=jnp.float32)
    return total.astype(jnp.bfloat16)


def outer_sum(left, right):
    return lax.dot_general(left, right, contract_first, preferred_element_type=jnp.float32)


def shards_plain(
    x_online,
    x_target,
    routes,
    gate_probs,
    expert_place,
    gate_online,
    up_online,
    down_online,
    gate_target,
    up_target,
    down_target,
):
    tok_rows, model_width = x_online.shape
    dp_count = lax.axis_size("dp")
    expert_count = lax.axis_size("expert")
    unit_count = dp_count * expert_count
    experts = expert_place.shape[0]
    capacity = 2 * ((2 * tok_rows + experts - 1) // experts)
    half_cap = capacity // 2
    half_width = gate_online.shape[2]
    chosen = routes.reshape(-1)
    onehot = (chosen[:, None] == jnp.arange(experts, dtype=jnp.int32)[None, :]).astype(jnp.int32)
    before = jnp.cumsum(onehot, axis=0) - onehot
    position = jnp.sum(before * onehot, axis=1)
    slot_place = jnp.sum(onehot * expert_place[None, :], axis=1)
    flat_slot = (2 * slot_place + position // half_cap) * half_cap + position % half_cap
    owner_token = jnp.arange(2 * tok_rows, dtype=jnp.int32) // 2

    def to_units(source):
        blank_rows = jnp.zeros((unit_count * half_cap, model_width), source.dtype)
        return (
            blank_rows.at[flat_slot]
            .set(source)
            .reshape(dp_count, expert_count, half_cap, model_width)
        )

    def from_units(block):
        picked = block.reshape(unit_count * half_cap, model_width)[flat_slot]
        return picked.astype(jnp.float32).reshape(tok_rows, 2, model_width)

    partner = swapped(
        (gate_online, up_online, down_online, gate_target, up_target, down_target), "expert", 0
    )
    gate_full = jnp.concatenate([gate_online[0], partner[0][0]], axis=1)
    up_full = jnp.concatenate([up_online[0], partner[1][0]], axis=1)
    down_full = jnp.concatenate([down_online[0], partner[2][0]], axis=0)
    gate_tfull = jnp.concatenate([gate_target[0], partner[3][0]], axis=1)
    up_tfull = jnp.concatenate([up_target[0], partner[4][0]], axis=1)
    down_tfull = jnp.concatenate([down_target[0], partner[5][0]], axis=0)
    recv_online, recv_target = (
        lax.all_to_all(
            lax.all_to_all(
                to_units(x_online[owner_token]), "dp", split_axis=0, concat_axis=0, tiled=True
            ),
            "expert",
            split_axis=1,
            concat_axis=1,
            tiled=True,
        ),
        lax.all_to_all(
            lax.all_to_all(
                to_units(x_target[owner_token]), "dp", split_axis=0, concat_axis=0, tiled=True
            ),
            "expert",
            split_axis=1,
            concat_axis=1,
            tiled=True,
        ),
    )
    unit_shape = recv_online.shape
    inputs_online = recv_online.reshape(-1, model_width)
    inputs_target = recv_target.reshape(-1, model_width)
    pre_gate, pre_up, hidden = hidden_forward(inputs_online, gate_full, up_full)
    out_online = jnp.dot(hidden, down_full, preferred_element_type=jnp.float32).astype(jnp.bfloat16)
    hidden_target = hidden_forward(inputs_target, gate_tfull, up_tfull)[2]
    out_target = jnp.dot(hidden_target, down_tfull, preferred_element_type=jnp.float32).astype(
        jnp.bfloat16
    )
    back_online, back_target = (
        lax.all_to_all(
            lax.all_to_all(
                out_online.reshape(unit_shape), "dp", split_axis=0, concat_axis=0, tiled=True
            ),
            "expert",
            split_axis=1,
            concat_axis=1,
            tiled=True,
        ),
        lax.all_to_all(
            lax.all_to_all(
                out_target.reshape(unit_shape), "dp", split_axis=0, concat_axis=0, tiled=True
            ),
            "expert",
            split_axis=1,
            concat_axis=1,
            tiled=True,
        ),
    )
    y_online = jnp.sum(from_units(back_online) * gate_probs[:, :, None], axis=1)
    y_target = jnp.sum(from_units(back_target) * gate_probs[:, :, None], axis=1)
    cotangent = (
        (gate_probs[:, :, None] * (y_online - y_target)[:, None, :])
        .astype(jnp.bfloat16)
        .reshape(2 * tok_rows, model_width)
    )
    cot_recv = lax.all_to_all(
        lax.all_to_all(to_units(cotangent), "dp", split_axis=0, concat_axis=0, tiled=True),
        "expert",
        split_axis=1,
        concat_axis=1,
        tiled=True,
    )
    cot_rows = cot_recv.reshape(-1, model_width)
    d_gate, d_up = hidden_grads(cot_rows, pre_gate, pre_up, down_full)
    d_rows = input_rows(d_gate, d_up, gate_full, up_full)
    back_grads = lax.all_to_all(
        lax.all_to_all(d_rows.reshape(unit_shape), "dp", split_axis=0, concat_axis=0, tiled=True),
        "expert",
        split_axis=1,
        concat_axis=1,
        tiled=True,
    )
    input_grad = jnp.sum(from_units(back_grads), axis=1).astype(jnp.bfloat16)
    g_gate = outer_sum(inputs_online, d_gate)
    g_up = outer_sum(inputs_online, d_up)
    g_down = outer_sum(hidden, cot_rows)
    sent = (
        swapped(g_gate[:, half_width:].astype(jnp.bfloat16), "expert", 0).astype(jnp.float32),
        swapped(g_up[:, half_width:].astype(jnp.bfloat16), "expert", 0).astype(jnp.float32),
        swapped(g_down[half_width:].astype(jnp.bfloat16), "expert", 0).astype(jnp.float32),
    )
    grad_gate = g_gate[:, :half_width] + sent[0]
    grad_up = g_up[:, :half_width] + sent[1]
    grad_down = g_down[:half_width] + sent[2]
    return (
        input_grad,
        grad_gate.astype(jnp.bfloat16)[None],
        grad_up.astype(jnp.bfloat16)[None],
        grad_down.astype(jnp.bfloat16)[None],
    )


MESH = pl.DeviceIdType.MESH
F32 = jnp.float32
BF16 = jnp.bfloat16


def dot(left, right, dims=(((1,), (0,)), ((), ()))):
    return lax.dot_general(left, right, dims, preferred_element_type=F32)


def step_kernel(
    slots,
    n_ex,
    cap,
    flat_ref,
    flat_t_ref,
    probs_ref,
    xo_ref,
    xt_ref,
    w0_ref,
    w1_ref,
    w2_ref,
    w3_ref,
    w4_ref,
    w5_ref,
    ig_ref,
    gg_ref,
    gu_ref,
    gd_ref,
    wg,
    wu,
    wd,
    sx,
    rx,
    pd,
    pr,
    ret,
    rc,
    pre_g,
    pre_u,
    hid,
    dgu,
    w_sem,
    send_sem,
    recv_sem,
    fsend_sem,
    frecv_sem,
    ysend_sem,
    yrecv_sem,
    bsend_sem,
    brecv_sem,
):
    tok, width = xo_ref.shape
    rows = slots * cap
    half = wg.shape[2]
    tile = 512
    dp, ex = lax.axis_index("dp"), lax.axis_index("expert")
    side = lax.rem(ex, 2)
    me = lax.div(dp * n_ex + ex, 2)
    partner = (dp, ex + 1 - 2 * side)

    planes = n_ex // 2
    group = slots // planes
    near, window = slots // 2, 5

    def other(i):
        mask = lax.rem(i, group) * planes + lax.div(i, group)
        slot, power = 0, 1
        while power < slots:
            bit = lax.rem(lax.rem(lax.div(me, power), 2) + lax.rem(lax.div(mask, power), 2), 2)
            slot, power = slot + bit * power, 2 * power
        return slot

    def peer(slot):
        unit = 2 * slot + side
        return (lax.div(unit, n_ex), lax.rem(unit, n_ex))

    def chunk(index):
        return pl.ds(pl.multiple_of(index * cap, cap), cap)

    barrier = pltpu.get_barrier_semaphore()

    def greet(o, carry):
        pl.semaphore_signal(
            barrier, inc=1, device_id=peer(other(o)), device_id_type=MESH
        )
        return carry

    lax.fori_loop(1, slots, greet, 0)
    pl.semaphore_signal(barrier, inc=1, device_id=partner, device_id_type=MESH)

    weight_copies = [
        pltpu.make_async_copy(source, target, w_sem.at[i])
        for i, (source, target) in enumerate(
            [
                (w0_ref, wg.at[0]),
                (w1_ref, wu.at[0]),
                (w2_ref, wd.at[0]),
                (w3_ref, wg.at[1]),
                (w4_ref, wu.at[1]),
                (w5_ref, wd.at[1]),
            ]
        )
    ]
    for copy in weight_copies:
        copy.start()

    def one_hot(compare):
        return jnp.where(compare, 1.0, 0.0).astype(BF16)

    row_iota = lax.broadcasted_iota(jnp.int32, (rows, tok), 0)
    put = [one_hot(row_iota == flat_t_ref[k : k + 1, :]) for k in range(2)]
    put_any = one_hot((row_iota == flat_t_ref[0:1, :]) | (row_iota == flat_t_ref[1:2, :]))
    col_iota = lax.broadcasted_iota(jnp.int32, (tok, rows), 1)
    take = [one_hot(col_iota == flat_ref[:, k : k + 1]) for k in range(2)]
    take_any = one_hot((col_iota == flat_ref[:, 0:1]) | (col_iota == flat_ref[:, 1:2]))

    def columns(body, low=0, high=width):
        def step(i, carry):
            body(pl.ds(pl.multiple_of(i * tile, tile), tile))
            return carry

        lax.fori_loop(low // tile, high // tile, step, 0)

    middle = width // 2
    span = [(0, middle), (middle, width)]

    def part_of(net):
        return pl.ds(*(((net % 2) * middle, middle) if net >= 2 else (0, width)))

    def each(low, body, high=slots):
        def step(o, carry):
            body(o)
            return carry

        lax.fori_loop(low, high, step, 0)

    def each_down(low, body):
        each(0, lambda o: body(slots - 1 - o), slots - low)

    def out_copy(net, dst, o):
        to = other(o)
        return pltpu.make_async_remote_copy(
            src_ref=sx.at[min(net, 2), chunk(to), part_of(net)],
            dst_ref=dst.at[0, chunk(o), part_of(net)],
            send_sem=send_sem.at[net, o],
            recv_sem=recv_sem.at[net, o],
            device_id=peer(to),
            device_id_type=MESH,
        )

    def fwd_copy(net, dst, o):
        return pltpu.make_async_remote_copy(
            src_ref=dst.at[0, chunk(o), part_of(net)],
            dst_ref=dst.at[1, chunk(o), part_of(net)],
            send_sem=fsend_sem.at[net, o],
            recv_sem=frecv_sem.at[net, o],
            device_id=partner,
            device_id_type=MESH,
        )

    def start_near(net, dst):
        each(1, lambda o: out_copy(net, dst, o).start(), near)
        dst[0, 0:cap, part_of(net)] = sx[min(net, 2), chunk(me), part_of(net)]
        fwd_copy(net, dst, 0).start()

    def start_far(net, dst):
        each(near, lambda o: out_copy(net, dst, o).start(), near + window)

    def relay(net, dst, then=None):
        def pass_on(o):
            out_copy(net, dst, o).wait_recv()
            fwd_copy(net, dst, o).start()

        def far(o):
            pass_on(o)
            out_copy(net, dst, o).wait_send()
            out_copy(net, dst, o + window).start()

        def last(o):
            pass_on(o)
            out_copy(net, dst, o).wait_send()
            if then is not None:
                out_copy(*then, o - (slots - window - near)).start()

        each(1, pass_on, near)
        if then is not None:
            start_near(*then)
        each(near, far, slots - window)
        each(slots - window, last)

    def arrived(net, dst):
        each(0, lambda o: fwd_copy(net, dst, o).wait_recv())

    def scatter_end(net, dst):
        each(0, lambda o: fwd_copy(net, dst, o).wait_send())
        each(1, lambda o: out_copy(net, dst, o).wait_send(), near)

    def half_of(turn):
        return pl.ds((turn % 2) * middle, middle)

    def pair_copy(turn, o):
        return pltpu.make_async_remote_copy(
            src_ref=pd.at[1, chunk(o), half_of(turn)],
            dst_ref=pr.at[turn // 2, chunk(o), half_of(turn)],
            send_sem=ysend_sem.at[turn, o],
            recv_sem=yrecv_sem.at[turn, o],
            device_id=partner,
            device_id_type=MESH,
        )

    def back_copy(turn, o):
        return pltpu.make_async_remote_copy(
            src_ref=pd.at[0, chunk(o), half_of(turn)],
            dst_ref=ret.at[turn // 2, chunk(me), half_of(turn)],
            send_sem=bsend_sem.at[turn, o],
            recv_sem=brecv_sem.at[turn, o],
            device_id=peer(other(o)),
            device_id_type=MESH,
        )

    def add_part(turn, o):
        pair_copy(turn, o).wait_recv()
        cols = half_of(turn)
        total = pd[0, chunk(o), cols].astype(F32) + pr[turn // 2, chunk(o), cols].astype(F32)
        return total.astype(BF16)

    def give_back(turn):
        def body(o):
            pd[0, chunk(o), half_of(turn)] = add_part(turn, o)
            back_copy(turn, o).start()

        each_down(1, body)
        ret[turn // 2, chunk(me), half_of(turn)] = add_part(turn, 0)

    def back_sent(turn):
        each(0, lambda o: pair_copy(turn, o).wait_send())
        each(1, lambda o: back_copy(turn, o).wait_send())

    def back_came(turn):
        each(1, lambda o: back_copy(turn, o).wait_recv())

    def place_online(cols):
        sx[0, :, cols] = dot(put_any, xo_ref[:, cols]).astype(BF16)

    def place_target(cols):
        sx[1, :, cols] = dot(put_any, xt_ref[:, cols]).astype(BF16)

    columns(place_online)
    pl.semaphore_wait(barrier, slots)
    start_far(0, rx.at[0])
    start_near(0, rx.at[0])
    columns(place_target)
    for copy in weight_copies:
        copy.wait()
    relay(0, rx.at[0], (1, rx.at[1]))
    relay(1, rx.at[1])

    def forward(net, part):
        gate = dot(rx[net, part], wg[net])
        up = dot(rx[net, part], wu[net])
        hid[net, part] = (gate * jax.nn.sigmoid(gate) * up).astype(BF16)
        if net == 0:
            pre_g[part] = gate
            pre_u[part] = up

    forward(0, 0)
    arrived(0, rx.at[0])
    forward(0, 1)
    forward(1, 0)
    arrived(1, rx.at[1])
    forward(1, 1)

    for side_part in (1, 0):

        def outputs(cols, part=side_part):
            diff = dot(hid[0, part], wd[0, :, cols]) - dot(hid[1, part], wd[1, :, cols])
            pd[part, :, cols] = diff.astype(BF16)

        for turn in (0, 1):
            columns(outputs, *span[turn])
            if side_part == 1:
                each_down(0, lambda o, turn=turn: pair_copy(turn, o).start())
    give_back(0)
    give_back(1)

    p0, p1 = probs_ref[:, 0:1], probs_ref[:, 1:2]

    def cotangents(cols):
        back = ret[0, :, cols]
        diff = p0 * dot(take[0], back) + p1 * dot(take[1], back)
        cot0, cot1 = (p0 * diff).astype(BF16), (p1 * diff).astype(BF16)
        sx[2, :, cols] = (dot(put[0], cot0) + dot(put[1], cot1)).astype(BF16)

    back_came(0)
    columns(cotangents, *span[0])
    start_far(2, rc)
    start_near(2, rc)
    back_came(1)
    columns(cotangents, *span[1])
    relay(2, rc, (3, rc))
    relay(3, rc)
    scatter_end(0, rx.at[0])
    scatter_end(1, rx.at[1])
    back_sent(0)
    back_sent(1)

    def hidden_back(part):
        d_hidden = dot(rc[part], wd[0], contract_last)
        gate, up = pre_g[part], pre_u[part]
        sig = jax.nn.sigmoid(gate)
        dgu[0, part] = (d_hidden * up * sig * (1.0 + gate * (1.0 - sig))).astype(BF16)
        dgu[1, part] = (d_hidden * (gate * sig)).astype(BF16)

    hidden_back(0)
    arrived(2, rc)
    arrived(3, rc)
    hidden_back(1)
    for side_part in (1, 0):

        def row_grads(cols, part=side_part):
            total = dot(dgu[0, part], wg[0, cols, :], contract_last)
            total = total + dot(dgu[1, part], wu[0, cols, :], contract_last)
            pd[part, :, cols] = total.astype(BF16)

        for turn in (2, 3):
            columns(row_grads, *span[turn - 2])
            if side_part == 1:
                each_down(0, lambda o, turn=turn: pair_copy(turn, o).start())
    give_back(2)
    give_back(3)

    def weight_grads(cols):
        for index, target in ((0, gg_ref), (1, gu_ref)):
            total = dot(rx[0, 0, :, cols], dgu[index, 0], contract_first)
            total = total + dot(rx[0, 1, :, cols], dgu[index, 1], contract_first)
            target[cols, :] = total.astype(BF16)
        total = dot(hid[0, 0], rc[0, :, cols], contract_first)
        total = total + dot(hid[0, 1], rc[1, :, cols], contract_first)
        gd_ref[:, cols] = total.astype(BF16)

    columns(weight_grads)
    scatter_end(2, rc)
    scatter_end(3, rc)
    back_came(2)

    def inputs_grad(cols):
        ig_ref[:, cols] = dot(take_any, ret[1, :, cols]).astype(BF16)

    columns(inputs_grad, *span[0])
    back_came(3)
    columns(inputs_grad, *span[1])
    back_sent(2)
    back_sent(3)


def shards(
    x_online,
    x_target,
    routes,
    gate_probs,
    expert_place,
    gate_online,
    up_online,
    down_online,
    gate_target,
    up_target,
    down_target,
):
    tok, width = x_online.shape
    slots = expert_place.shape[0]
    n_ex = lax.axis_size("expert")
    cap = 2 * ((2 * tok + slots - 1) // slots)
    rows = slots * cap
    half = gate_online.shape[2]
    paired = 2 * slots == lax.axis_size("dp") * n_ex and n_ex % 2 == 0
    halving = slots & (slots - 1) == 0 and n_ex & (n_ex - 1) == 0
    if cap % 16 or width % 1024 or slots < 16 or not (paired and halving):
        return shards_plain(
            x_online,
            x_target,
            routes,
            gate_probs,
            expert_place,
            gate_online,
            up_online,
            down_online,
            gate_target,
            up_target,
            down_target,
        )
    chosen = routes.reshape(-1)
    onehot = (chosen[:, None] == jnp.arange(slots, dtype=jnp.int32)[None, :]).astype(jnp.int32)
    before = jnp.cumsum(onehot, axis=0) - onehot
    flat = jnp.sum((before + cap * expert_place[None, :]) * onehot, axis=1).reshape(tok, 2)
    vmem = pl.BlockSpec(memory_space=pltpu.VMEM)
    hbm = pl.BlockSpec(memory_space=pl.ANY)
    dma = pltpu.SemaphoreType.DMA
    outs = pl.pallas_call(
        functools.partial(step_kernel, slots, n_ex, cap),
        out_shape=(
            jax.ShapeDtypeStruct((tok, width), BF16),
            jax.ShapeDtypeStruct((width, half), BF16),
            jax.ShapeDtypeStruct((width, half), BF16),
            jax.ShapeDtypeStruct((half, width), BF16),
        ),
        in_specs=[vmem] * 5 + [hbm] * 6,
        out_specs=(vmem,) * 4,
        scratch_shapes=[
            pltpu.VMEM((2, width, half), BF16),
            pltpu.VMEM((2, width, half), BF16),
            pltpu.VMEM((2, half, width), BF16),
            pltpu.VMEM((3, rows, width), BF16),
            pltpu.VMEM((2, 2, rows, width), BF16),
            pltpu.VMEM((2, rows, width), BF16),
            pltpu.VMEM((2, rows, width), BF16),
            pltpu.VMEM((2, rows, width), BF16),
            pltpu.VMEM((2, rows, width), BF16),
            pltpu.VMEM((2, rows, half), F32),
            pltpu.VMEM((2, rows, half), F32),
            pltpu.VMEM((2, 2, rows, half), BF16),
            pltpu.VMEM((2, 2, rows, half), BF16),
            dma((6,)),
            dma((4, slots)),
            dma((4, slots)),
            dma((4, slots)),
            dma((4, slots)),
            dma((4, slots)),
            dma((4, slots)),
            dma((4, slots)),
            dma((4, slots)),
        ],
        compiler_params=pltpu.CompilerParams(
            collective_id=0, has_side_effects=True, vmem_limit_bytes=60 * 2**20
        ),
    )(
        flat,
        flat.T,
        gate_probs,
        x_online,
        x_target,
        gate_online[0],
        up_online[0],
        down_online[0],
        gate_target[0],
        up_target[0],
        down_target[0],
    )
    return (outs[0], outs[1][None], outs[2][None], outs[3][None])


def solution(mesh):
    in_specs = (
        P(("dp", "expert"), None),
        P(("dp", "expert"), None),
        P(("dp", "expert"), None),
        P(("dp", "expert"), None),
        P(),
        P(("dp", "expert"), None, None),
        P(("dp", "expert"), None, None),
        P(("dp", "expert"), None, None),
        P(("dp", "expert"), None, None),
        P(("dp", "expert"), None, None),
        P(("dp", "expert"), None, None),
    )
    out_specs = (
        P(("dp", "expert"), None),
        P(("dp", "expert"), None, None),
        P(("dp", "expert"), None, None),
        P(("dp", "expert"), None, None),
    )
    return jax.shard_map(shards, mesh=mesh, in_specs=in_specs, out_specs=out_specs, check_vma=False)
```
